32 devices in a mesh: grp: 4 (over y, core), seq: 8 (over z, x).
Axes of the slice: x: 2, y: 2, z: 4, core: 2. Of those that a mesh axis runs over, the one named last changes fastest.
Arguments:
- queries: bfloat16 [16384, 512], P(('grp', 'seq')), may hold values from -8 to 8
- keys: bfloat16 [16384, 512], P(('grp', 'seq')), may hold values from -4.5 to 4.5
- values: bfloat16 [16384, 512], P(('grp', 'seq')), may hold values from -6 to 6
- resid: bfloat16 [16384, 1024], P(('grp', 'seq')), may hold values from -54 to 54
- w_out: bfloat16 [512, 1024], replicated, may hold values from -2 to 2
- block_lang: int32 [256], P(('grp', 'seq')), may hold values from 0 to 11, as said below
- w_down: bfloat16 [12, 1024, 384], P('grp', 'seq'), may hold values from -0.1875 to 0.1875
- w_up: bfloat16 [12, 384, 1024], P('grp', None, 'seq'), may hold values from -0.3125 to 0.3125
- bias_down: bfloat16 [12, 384], P('grp'), may hold values from -4 to 4
- cotangent: bfloat16 [16384, 1024], P(('grp', 'seq')), may hold values from -6 to 6
Outputs:
- grad_down: float32 [1024, 12, 384], P('seq', 'grp')
The draws below stay inside these ranges and needn't reach their ends.
Inputs may be any that keep to these rules, and one draw needn't show every extreme that they name: Block b holds tokens b * 64 to (b + 1) * 64 - 1, and its language's owner group is block_lang[b] // 3. Of the 8 blocks of one device (blocks d * 8 to (d + 1) * 8 - 1), at most 2 have the same owner group; for every index along seq, some owner group has a block from the device of that index in every group.
All inputs are finite; a program needn't handle non-finite values.
Results may differ from the reference program's by a relative error of at most 0.022.
Values may be sent and summed in bfloat16 or wider, within the bound.
No kernel may reach another device: no remote copies, remote signals or barrier semaphores. Data moves between devices by JAX's collectives and lax.ppermute only.
A program may use at most 128 MiB of HBM per device.

```python
import math
import jax
import jax.numpy as jnp
from jax import lax

D = 1024
HEADS = 8
HD = 64
HQ = 512
R = 384
LANG_GRP = 3
WINDOW = 256
BLK = 64
BPD = 8
TOK_DEV = 512
LEN = 4096
TOKENS = 16384
BLOCKS = 256
LANGS = 12
N_GRP = 4
N_SEQ = 8


def draw_queries(key, part):
    width_q = HEADS * HD
    sampled = jnp.clip(jax.random.normal(jax.random.fold_in(key, 1), (TOKENS, width_q), jnp.float32), -6.0, 6.0)
    return sampled.astype(jnp.bfloat16)


def draw_keys(key, part):
    width_q = HEADS * HD
    sampled = jnp.clip(jax.random.normal(jax.random.fold_in(key, 2), (TOKENS, width_q), jnp.float32), -4.5, 4.5)
    return sampled.astype(jnp.bfloat16)


def draw_resid(key, part):
    sampled = jnp.clip(jax.random.normal(jax.random.fold_in(key, 3), (TOKENS, D), jnp.float32), -6.0, 6.0)
    return sampled.astype(jnp.bfloat16)


def draw_block_lang(key, part):
    group_count = TOKENS // LEN
    seq_count = LEN // TOK_DEV
    dev_count = group_count * seq_count
    cap_each = max(1, BPD // group_count)
    pool = group_count * cap_each
    pool_group = jnp.arange(pool) // cap_each
    group_rank = jax.random.permutation(jax.random.fold_in(key, 21), group_count)
    forced = jax.random.randint(jax.random.fold_in(key, 22), (seq_count,), 0, group_count)
    raw_scores = jax.random.randint(jax.random.fold_in(key, 23), (dev_count, pool), 0, 1 << 20)
    scored = raw_scores // (group_rank[pool_group][None, :] + 1)
    seq_of = jnp.arange(dev_count) % seq_count
    forced_hit = (forced[seq_of][:, None] == pool_group[None, :]).astype(jnp.int32)
    scored = (scored + forced_hit * (1 << 21)) * pool + jnp.arange(pool)[None, :]
    chosen = lax.top_k(scored, BPD)[1]
    shuffle_keys = jax.random.randint(jax.random.fold_in(key, 24), (dev_count, BPD), 0, 1 << 20) * BPD + jnp.arange(BPD)[None, :]
    placing = jnp.argsort(shuffle_keys, axis=1)
    picked = jnp.take_along_axis(chosen, placing, axis=1)
    groups_picked = picked // cap_each
    language = groups_picked * LANG_GRP + jax.random.randint(jax.random.fold_in(key, 25), (dev_count, BPD), 0, LANG_GRP)
    return language.reshape(BLOCKS).astype(jnp.int32)


def steps_of(own_key, dims, split, low, largest):
    gain = 1.0
    for position, parts in split:
        draws = jax.random.uniform(jax.random.fold_in(jax.random.fold_in(own_key, 6), position), (parts,), jnp.float32, low / len(split), largest / len(split))
        gain = gain * jnp.repeat(jnp.exp(draws), dims[position] // parts).reshape((-1,) + (1,) * (len(dims) - 1 - position))
    return gain


def noise(own_key, dims, width, limit, pieces=(), kind=jnp.bfloat16):
    array = jax.random.normal(own_key, dims, jnp.float32) * width
    if len(pieces) > 0:
        array = steps_of(own_key, dims, pieces, -0.22, 0.18) * array
    return jnp.clip(array, min=-limit, max=limit).astype(kind)


def setup_inputs(seed: int = 0) -> dict:
    streams_of = jax.random.split(jax.random.key(seed), 11)
    queries = draw_queries(jax.random.fold_in(streams_of[10], 71), 0)
    keys = draw_keys(jax.random.fold_in(streams_of[10], 71), 0)
    values = noise(streams_of[2], (TOKENS, HQ), 1.0, 6.0, ((0, 32),))
    resid = draw_resid(jax.random.fold_in(streams_of[10], 71), 0)
    w_out = noise(streams_of[4], (HQ, D), 0.35, 2.0)
    block_lang = draw_block_lang(jax.random.fold_in(streams_of[10], 71), 0)
    w_down = noise(streams_of[6], (LANGS, D, R), D ** -0.5, 0.1875, ((0, 4), (1, 8)))
    w_up = noise(streams_of[7], (LANGS, R, D), R ** -0.5, 0.3125, ((0, 4), (2, 8)))
    bias_down = noise(streams_of[8], (LANGS, R), 1.0, 4.0, ((0, 4),))
    cotangent = noise(streams_of[9], (TOKENS, D), 1.0, 6.0, ((0, 32),))
    return {"queries": queries, "keys": keys, "values": values, "resid": resid, "w_out": w_out, "block_lang": block_lang, "w_down": w_down, "w_up": w_up, "bias_down": bias_down, "cotangent": cotangent}


EPSILON = 1e-05

def gelu_slope(pre_act):
    return jax.vjp(jax.nn.gelu, pre_act)[1](jnp.ones_like(pre_act))[0]

def normalize(block_rows):
    widened = block_rows.astype(jnp.float32)
    center = widened - lax.optimization_barrier(jnp.mean(widened, axis=-1, keepdims=True))
    spread = lax.optimization_barrier(jnp.mean(center * center, axis=-1, keepdims=True))
    return (center * lax.rsqrt(spread + EPSILON)).astype(jnp.bfloat16)

def attend(q_rows, k_rows, v_rows, first_blk):
    length = q_rows.shape[0]
    key_span = k_rows.shape[0]
    q_heads = q_rows.astype(jnp.float32).reshape(length, HEADS, HD)
    k_heads = k_rows.astype(jnp.float32).reshape(key_span, HEADS, HD)
    v_heads = v_rows.astype(jnp.float32).reshape(key_span, HEADS, HD)
    scores = jnp.einsum('qhd,khd->hqk', q_heads, k_heads) * HD ** (-0.5)
    q_pos = jnp.arange(length)[:, None] + WINDOW
    k_pos = jnp.arange(key_span)[None, :]
    allowed = (k_pos <= q_pos) & (k_pos > q_pos - WINDOW) & ((k_pos >= WINDOW) | jnp.logical_not(first_blk))
    scores = jnp.where(allowed[None], scores, -1e+30)
    row_max = lax.optimization_barrier(jnp.max(scores, axis=-1, keepdims=True))
    weights = jnp.exp(scores - row_max) * allowed[None]
    softmax_w = (weights / lax.optimization_barrier(jnp.sum(weights, axis=-1, keepdims=True))).astype(jnp.bfloat16)
    context = jnp.einsum('hqk,khd->qhd', softmax_w.astype(jnp.float32), v_heads)
    return context.astype(jnp.bfloat16).reshape(length, HEADS * HD)

def reference(queries, keys, values, resid, w_out, block_lang, w_down, w_up, bias_down, cotangent):
    shard_count = TOKENS // TOK_DEV
    width_q = HEADS * HD
    q_shards = queries.reshape(shard_count, TOK_DEV, width_q)
    k_shards = keys.reshape(shard_count, TOK_DEV, width_q)
    v_shards = values.reshape(shard_count, TOK_DEV, width_q)
    r_shards = resid.reshape(shard_count, TOK_DEV, D)
    k_prev = jnp.concatenate([jnp.zeros_like(k_shards[:1]), k_shards[:-1]], axis=0)[:, TOK_DEV - WINDOW:]
    v_prev = jnp.concatenate([jnp.zeros_like(v_shards[:1]), v_shards[:-1]], axis=0)[:, TOK_DEV - WINDOW:]
    first_blk = jnp.arange(shard_count) % N_SEQ == 0

    def one_shard(shard_item):
        q_rows, k_rows, v_rows, k_rim, v_rim, first_one, r_rows = shard_item
        context = attend(q_rows, jnp.concatenate([k_rim, k_rows], axis=0), jnp.concatenate([v_rim, v_rows], axis=0), first_one)
        mixed_rows = r_rows.astype(jnp.float32) + jnp.dot(context, w_out, preferred_element_type=jnp.float32)
        return mixed_rows.astype(jnp.bfloat16)
    hidden = lax.map(one_shard, (q_shards, k_shards, v_shards, k_prev, v_prev, first_blk, r_shards))
    hidden_blocks = hidden.reshape(N_GRP, N_SEQ, BPD, BLK, D).transpose(1, 0, 2, 3, 4).reshape(N_SEQ, N_GRP * BPD, BLK, D)
    cot_blocks = cotangent.reshape(N_GRP, N_SEQ, BPD, BLK, D).transpose(1, 0, 2, 3, 4).reshape(N_SEQ, N_GRP * BPD, BLK, D)
    lang_blocks = block_lang.reshape(N_GRP, N_SEQ, BPD).transpose(1, 0, 2).reshape(N_SEQ, N_GRP * BPD).astype(jnp.int32)
    inv_scale = 1.0 / math.sqrt(TOK_DEV * N_SEQ)

    def one_block(running, block_item):
        block_rows, block_cot, language = block_item
        normed = normalize(block_rows)
        pre_act = jnp.dot(normed, w_down[language], preferred_element_type=jnp.float32) + bias_down[language].astype(jnp.float32)
        back_proj = jnp.dot(block_cot, w_up[language].T, preferred_element_type=jnp.float32)
        gate_grad = (gelu_slope(pre_act) * back_proj).astype(jnp.bfloat16)
        update = jnp.dot(normed.T, gate_grad, preferred_element_type=jnp.float32)
        return (running.at[language].add(update), None)

    def one_seq(grand_total, seq_item):
        empty_acc = jnp.zeros((LANGS, D, R), jnp.float32)
        partial_sum = lax.scan(one_block, empty_acc, seq_item)[0]
        rounded = lax.optimization_barrier((partial_sum * inv_scale).astype(jnp.bfloat16))
        return (grand_total + rounded.astype(jnp.float32), None)
    grand_total = lax.scan(one_seq, jnp.zeros((LANGS, D, R), jnp.float32), (hidden_blocks, cot_blocks, lang_blocks))[0]
    return jnp.transpose(grand_total, (1, 0, 2))
```

```python
import functools
import math

import jax
import jax.numpy as jnp
from jax import lax
from jax.experimental import pallas as pl
from jax.experimental.pallas import tpu as pltpu
from jax.sharding import PartitionSpec as P

HD = 64
WINDOW = 256
EPSILON = 1e-05
TILE = 128
LANES = 128
MARK = 16
NEG = -1e30


VMEM = pl.BlockSpec(memory_space=pltpu.VMEM)
SMEM = pl.BlockSpec(memory_space=pltpu.SMEM)


def ring_order(size):
    return list(range(0, size, 2)) + [i for i in range(size - 1, 0, -1) if i % 2]


def ring_pairs(size, step):
    order = ring_order(size)
    return [(order[i], order[(i + step) % size]) for i in range(size)]


def ring_place(index, size):
    half = index // 2
    return jnp.where(index % 2 == 0, half, size - 1 - half)


def ring_member(place, size):
    ups = (size + 1) // 2
    return jnp.where(place < ups, 2 * place, 2 * (size - place) - 1)


def peer_of(index, step, size):
    if size & (size - 1) == 0:
        return index ^ step
    return (index + step) % size


def dot(a, b, dims):
    return lax.dot_general(a, b, (dims, ((), ())), preferred_element_type=jnp.float32)


def attend(q_ref, k_win, v_win, ctx_ref, row0, bias):
    width = q_ref.shape[1]
    group = min(width, 256)
    heads = group // HD
    for col0 in range(0, width, group):
        q_part = q_ref[row0 : row0 + TILE, col0 : col0 + group] * jnp.bfloat16(HD**-0.5)
        lane_head = lax.broadcasted_iota(jnp.int32, q_part.shape, 1) // HD
        q_diag = jnp.concatenate(
            [jnp.where(lane_head == h, q_part, jnp.zeros_like(q_part)) for h in range(heads)], axis=0
        )
        keys = k_win[:, col0 : col0 + group]
        vals = v_win[:, col0 : col0 + group]
        scores = dot(q_diag, keys, ((1,), (1,)))
        scores = scores.reshape(heads, TILE, scores.shape[1]) + bias[None]
        top = jnp.max(scores, axis=-1, keepdims=True)
        weights = jnp.exp(scores - top)
        total = jnp.sum(weights, axis=-1, keepdims=True)
        soft = (weights / total).astype(jnp.bfloat16).reshape(heads * TILE, -1)
        mixed = dot(soft, vals, ((1,), (0,)))
        picked = jnp.zeros((TILE, group), jnp.float32)
        for h in range(heads):
            picked = jnp.where(lane_head == h, mixed[h * TILE : (h + 1) * TILE], picked)
        ctx_ref[row0 : row0 + TILE, col0 : col0 + group] = picked.astype(jnp.bfloat16)


def window_bias():
    shape = (TILE, TILE + WINDOW)
    row = lax.broadcasted_iota(jnp.int32, shape, 0)
    col = lax.broadcasted_iota(jnp.int32, shape, 1)
    allowed = (col <= row + WINDOW) & (col > row)
    return jnp.where(allowed, 0.0, NEG).astype(jnp.float32), col


def finish_rows(ctx_ref, r_ref, wo_ref):
    hidden = (
        r_ref[...].astype(jnp.float32) + dot(ctx_ref[...], wo_ref[...], ((1,), (0,)))
    ).astype(jnp.bfloat16).astype(jnp.float32)
    center = hidden - jnp.mean(hidden, axis=-1, keepdims=True)
    spread = jnp.mean(center * center, axis=-1, keepdims=True)
    return (center * lax.rsqrt(spread + EPSILON)).astype(jnp.bfloat16)


def late_kernel(q_ref, k_ref, v_ref, r_ref, wo_ref, out_ref, ctx_ref):
    bias, _ = window_bias()
    for row0 in range(0, q_ref.shape[0], TILE):
        span = slice(row0, row0 + TILE + WINDOW)
        attend(q_ref, k_ref[span, :], v_ref[span, :], ctx_ref, row0, bias)
    out_ref[...] = finish_rows(ctx_ref, r_ref, wo_ref)


def block_for(lang_ref, owner, rank, lang_grp):
    block, local, seen = jnp.int32(0), jnp.int32(-1), jnp.int32(0)
    for b in range(lang_ref.shape[0]):
        lang = lang_ref[b]
        mine = lang // lang_grp == owner
        take = mine & (seen == rank)
        block = jnp.where(take, b, block)
        local = jnp.where(take, lang - owner * lang_grp, local)
        seen = seen + mine.astype(jnp.int32)
    return block, local


def early_kernel(
    groups, lang_grp, lang_ref, q_ref, rim_ref, k_ref, v_ref, r_ref, wo_ref, late_ref, *rest
):
    outs, (ctx_ref, kk_ref, vv_ref, rows_ref) = rest[:groups], rest[groups:]
    rows = q_ref.shape[0]
    width = q_ref.shape[1]
    kk_ref[:WINDOW, :] = rim_ref[:, :width]
    vv_ref[:WINDOW, :] = rim_ref[:, width:]
    kk_ref[WINDOW:, :] = k_ref[...]
    vv_ref[WINDOW:, :] = v_ref[...]
    bias, col = window_bias()
    first = lax.axis_index("seq") == 0
    for row0 in range(0, rows, TILE):
        span = slice(row0, row0 + TILE + WINDOW)
        shut = jnp.logical_and(first, col + row0 < WINDOW)
        attend(q_ref, kk_ref[span, :], vv_ref[span, :], ctx_ref, row0, jnp.where(shut, NEG, bias))
    blocks = lang_ref.shape[0]
    length = rows_ref.shape[1]
    done = finish_rows(ctx_ref, r_ref, wo_ref)
    split = rows // length
    rows_ref[:split] = done.reshape(split, length, -1)
    rows_ref[split:] = late_ref[...].reshape(blocks - split, length, -1)
    me = lax.axis_index("grp")
    for step, out_ref in enumerate(outs):
        owner = peer_of(me, step, groups)
        for j in range(out_ref.shape[0] // length):
            block, _ = block_for(lang_ref, owner, j, lang_grp)
            out_ref[j * length : (j + 1) * length, :] = rows_ref[block]


def pack_kernel(groups, lang_grp, lang_ref, c_ref, *outs):
    length = c_ref.shape[1]
    me = lax.axis_index("grp")
    for step, out_ref in enumerate(outs):
        owner = peer_of(me, step, groups)
        cap = (out_ref.shape[0] - MARK) // length
        row = lax.broadcasted_iota(jnp.int32, (MARK, out_ref.shape[1]), 0)
        mark = jnp.full(row.shape, -1.0, jnp.float32)
        for j in range(cap):
            block, local = block_for(lang_ref, owner, j, lang_grp)
            out_ref[j * length : (j + 1) * length, :] = c_ref[block]
            mark = jnp.where(row == j, local.astype(jnp.float32), mark)
        out_ref[cap * length :, :] = mark.astype(jnp.bfloat16)


def gelu_slope(v):
    rate = math.sqrt(2 / math.pi)
    square = v * v
    t = jnp.tanh(rate * v * (1.0 + 0.044715 * square))
    return 0.5 * (1.0 + t) + (0.5 * rate) * v * (1.0 - t * t) * (1.0 + (3 * 0.044715) * square)


def grad_kernel(groups, chunks, length, inv_scale, whole, *refs):
    refs = list(refs)
    take = lambda count: [refs.pop(0) for _ in range(count)]
    rows, cots = take(groups), take(groups)
    downs, ups = take(chunks), take(chunks)
    (bias_ref,) = take(1)
    x_ref, c_ref, g_ref = refs[-3:]
    outs = refs[:-3]
    part = rows[0].shape[0]
    lang_grp, units = bias_ref.shape
    width = x_ref.shape[1] // chunks
    for i in range(groups):
        span = slice(i * part, (i + 1) * part)
        if whole:
            x_ref[span, :] = rows[i][...]
            c_ref[span, :] = cots[i][:part, :]
            continue
        place = ring_place(lax.axis_index("seq"), chunks)
        for k in range(chunks):
            member = ring_member((place + k) % chunks, chunks)
            columns = pl.ds(pl.multiple_of(member * width, width), width)
            x_ref[span, k * width : (k + 1) * width] = rows[i][:, columns]
            c_ref[span, k * width : (k + 1) * width] = cots[i][:part, columns]
    pre, back = [], []
    for l in range(lang_grp):
        w_down = jnp.concatenate([d[l] for d in downs], axis=0)
        w_up = jnp.concatenate([u[l] for u in ups], axis=1)
        pre.append(
            dot(x_ref[...], w_down, ((1,), (0,))) + bias_ref[l : l + 1, :].astype(jnp.float32)
        )
        back.append(dot(c_ref[...], w_up, ((1,), (1,))))
    for i in range(groups):
        marks = cots[i][part:, :units].astype(jnp.float32)
        for j in range(part // length):
            span = slice(i * part + j * length, i * part + (j + 1) * length)
            lang = marks[j : j + 1, :]
            value, other = pre[0][span], back[0][span]
            for l in range(1, lang_grp):
                value = jnp.where(lang == l, pre[l][span], value)
                other = jnp.where(lang == l, back[l][span], other)
            gate = (gelu_slope(value) * other).astype(jnp.bfloat16)
            for l in range(lang_grp):
                g_ref[span, l * units : (l + 1) * units] = jnp.where(
                    lang == l, gate, jnp.zeros_like(gate)
                )
    at = 0
    for out_ref in outs:
        count = out_ref.shape[0]
        slab = dot(x_ref[:, at : at + count], g_ref[...], ((0,), (0,)))
        out_ref[...] = (slab * inv_scale).astype(out_ref.dtype)
        at += count


def cycle_gather(value, size, far):
    held = {0: value}
    half = size // 2
    for way in (-1, 1):
        moving = value
        for hop in range(1, half + (1 if way == far else 0)):
            moving = lax.ppermute(moving, "seq", ring_pairs(size, -way))
            held[(way * hop) % size] = moving
    return [held[k] for k in range(size)]


def cycle_reduce(parts, size, far):
    half = size // 2
    total = parts[0].astype(jnp.float32)
    for way in (1, -1):
        hops = half if way == far else half - 1
        moving = parts[(way * hops) % size]
        for hop in range(hops - 1, -1, -1):
            moving = lax.ppermute(moving, "seq", ring_pairs(size, way))
            if hop:
                mine = parts[(way * hop) % size]
                moving = (moving.astype(jnp.float32) + mine.astype(jnp.float32)).astype(mine.dtype)
        total = total + moving.astype(jnp.float32)
    return total


def body(queries, keys, values, resid, w_out, block_lang, w_down, w_up, bias_down, cotangent):
    tok_dev, width_q = queries.shape
    model = resid.shape[1]
    blocks = block_lang.shape[0]
    length = tok_dev // blocks
    groups = lax.axis_size("grp")
    size = lax.axis_size("seq")
    cap = max(1, blocks // groups)
    lang_grp, _, units = w_down.shape
    bf16 = jnp.bfloat16
    late = tok_dev - WINDOW

    edge = jnp.concatenate([keys[late:], values[late:]], axis=1)
    rim = lax.ppermute(edge, "seq", [(i, i + 1) for i in range(size - 1)])

    downs = cycle_gather(w_down, size, -1)
    ups = cycle_gather(w_up, size, 1)

    cot_out = pl.pallas_call(
        functools.partial(pack_kernel, groups, lang_grp),
        out_shape=[jax.ShapeDtypeStruct((cap * length + MARK, model), bf16)] * groups,
        in_specs=[SMEM, VMEM],
        out_specs=[VMEM] * groups,
        name="pack",
    )(block_lang, cotangent.reshape(blocks, length, model))

    def exchange(messages):
        got = [messages[0]]
        for step in range(1, groups):
            pairs = [(i, peer_of(i, step, groups)) for i in range(groups)]
            got.append(lax.ppermute(messages[step], "grp", pairs))
        return got

    cots = exchange(cot_out)

    def block_spec(shape, index):
        return pl.BlockSpec(shape, lambda i: index)

    full = lambda a: block_spec(a.shape, (0,) * a.ndim)
    half_q = late // WINDOW
    rows_late = pl.pallas_call(
        late_kernel,
        grid=(1,),
        out_shape=jax.ShapeDtypeStruct((late, model), bf16),
        in_specs=[
            block_spec((late, width_q), (half_q, 0)),
            full(keys),
            full(values),
            block_spec((late, model), (half_q, 0)),
            full(w_out),
        ],
        out_specs=block_spec((late, model), (0, 0)),
        scratch_shapes=[pltpu.VMEM((late, width_q), bf16)],
        name="late",
    )(queries, keys, values, resid, w_out)

    row_out = pl.pallas_call(
        functools.partial(early_kernel, groups, lang_grp),
        grid=(1,),
        out_shape=[jax.ShapeDtypeStruct((cap * length, model), bf16)] * groups,
        in_specs=[
            SMEM,
            block_spec((WINDOW, width_q), (0, 0)),
            full(rim),
            block_spec((WINDOW, width_q), (0, 0)),
            block_spec((WINDOW, width_q), (0, 0)),
            block_spec((WINDOW, model), (0, 0)),
            full(w_out),
            full(rows_late),
        ],
        out_specs=[block_spec((cap * length, model), (0, 0))] * groups,
        scratch_shapes=[
            pltpu.VMEM((WINDOW, width_q), bf16),
            pltpu.VMEM((2 * WINDOW, width_q), bf16),
            pltpu.VMEM((2 * WINDOW, width_q), bf16),
            pltpu.VMEM((blocks, length, model), bf16),
        ],
        name="early",
    )(block_lang, queries, rim, keys, values, resid, w_out, rows_late)
    rows = exchange(row_out)

    share = model // size
    whole = share % LANES != 0
    cells = lang_grp * units
    if whole:
        place = ring_place(lax.axis_index("seq"), size)
        at_offset = ring_member((place + jnp.arange(size)) % size, size)
        of_member = jnp.argsort(at_offset)
        stack = jnp.take(jnp.stack(downs), of_member, axis=0)
        downs = [stack.transpose(1, 0, 2, 3).reshape(lang_grp, model, units)]
        stack = jnp.take(jnp.stack(ups), of_member, axis=0)
        ups = [stack.transpose(1, 2, 0, 3).reshape(lang_grp, units, model)]
        out_rows = [model]
    else:
        out_rows = [share // 2] * (2 * size)
    tokens = groups * cap * length
    slabs = pl.pallas_call(
        functools.partial(
            grad_kernel, groups, len(downs), length, 1.0 / math.sqrt(tok_dev * size), whole
        ),
        out_shape=[jax.ShapeDtypeStruct((count, cells), bf16) for count in out_rows],
        in_specs=[VMEM] * (2 * groups + 2 * len(downs) + 1),
        out_specs=[VMEM] * len(out_rows),
        scratch_shapes=[
            pltpu.VMEM((tokens, model), bf16),
            pltpu.VMEM((tokens, model), bf16),
            pltpu.VMEM((tokens, cells), bf16),
        ],
        name="grads",
    )(*rows, *cots, *downs, *ups, bias_down)
    if whole:
        cut = jnp.take(slabs[0].reshape(size, 2, share // 2, cells), at_offset, axis=0)
        slabs = [cut[k, h] for k in range(size) for h in range(2)]
    upper = cycle_reduce(slabs[0::2], size, 1)
    lower = cycle_reduce(slabs[1::2], size, -1)
    return jnp.concatenate([upper, lower], axis=0).reshape(share, lang_grp, units)


def solution(mesh):
    in_specs = (
        P(("grp", "seq"), None),
        P(("grp", "seq"), None),
        P(("grp", "seq"), None),
        P(("grp", "seq"), None),
        P(),
        P(("grp", "seq")),
        P("grp", "seq", None),
        P("grp", None, "seq"),
        P("grp", None),
        P(("grp", "seq"), None),
    )
    out_specs = P("seq", "grp", None)
    return jax.shard_map(body, mesh=mesh, in_specs=in_specs, out_specs=out_specs, check_vma=False)
```

```python
import functools
import math

import jax
import jax.numpy as jnp
from jax import lax
from jax.experimental import pallas as pl
from jax.experimental.pallas import tpu as pltpu
from jax.sharding import PartitionSpec as P


HD = 64
WINDOW = 256
EPSILON = 1e-05
TILE = 128
LANES = 128
MARK = 16
NEG = -1e30


VMEM = pl.BlockSpec(memory_space=pltpu.VMEM)
SMEM = pl.BlockSpec(memory_space=pltpu.SMEM)


def ring_order(size):
    return list(range(0, size, 2)) + [i for i in range(size - 1, 0, -1) if i % 2]


def ring_pairs(size, step):
    order = ring_order(size)
    return [(order[i], order[(i + step) % size]) for i in range(size)]


def ring_place(index, size):
    half = index // 2
    return jnp.where(index % 2 == 0, half, size - 1 - half)


def ring_member(place, size):
    ups = (size + 1) // 2
    return jnp.where(place < ups, 2 * place, 2 * (size - place) - 1)


def peer_of(index, step, size):
    if size & (size - 1) == 0:
        return index ^ step
    return (index + step) % size


def dot(a, b, dims):
    return lax.dot_general(a, b, (dims, ((), ())), preferred_element_type=jnp.float32)


def attend(q_ref, k_win, v_win, ctx_ref, row0, bias):
    width = q_ref.shape[1]
    group = min(width, 256)
    heads = group // HD
    for col0 in range(0, width, group):
        q_part = q_ref[row0 : row0 + TILE, col0 : col0 + group] * jnp.bfloat16(HD**-0.5)
        lane_head = lax.broadcasted_iota(jnp.int32, q_part.shape, 1) // HD
        q_diag = jnp.concatenate(
            [jnp.where(lane_head == h, q_part, jnp.zeros_like(q_part)) for h in range(heads)], axis=0
        )
        keys = k_win[:, col0 : col0 + group]
        vals = v_win[:, col0 : col0 + group]
        scores = dot(q_diag, keys, ((1,), (1,)))
        scores = scores.reshape(heads, TILE, scores.shape[1]) + bias[None]
        top = jnp.max(scores, axis=-1, keepdims=True)
        weights = jnp.exp(scores - top)
        total = jnp.sum(weights, axis=-1, keepdims=True)
        soft = (weights / total).astype(jnp.bfloat16).reshape(heads * TILE, -1)
        mixed = dot(soft, vals, ((1,), (0,)))
        picked = jnp.zeros((TILE, group), jnp.float32)
        for h in range(heads):
            picked = jnp.where(lane_head == h, mixed[h * TILE : (h + 1) * TILE], picked)
        ctx_ref[row0 : row0 + TILE, col0 : col0 + group] = picked.astype(jnp.bfloat16)


def window_bias():
    shape = (TILE, TILE + WINDOW)
    row = lax.broadcasted_iota(jnp.int32, shape, 0)
    col = lax.broadcasted_iota(jnp.int32, shape, 1)
    allowed = (col <= row + WINDOW) & (col > row)
    return jnp.where(allowed, 0.0, NEG).astype(jnp.float32), col


def finish_rows(ctx_ref, r_ref, wo_ref):
    hidden = (
        r_ref[...].astype(jnp.float32) + dot(ctx_ref[...], wo_ref[...], ((1,), (0,)))
    ).astype(jnp.bfloat16).astype(jnp.float32)
    center = hidden - jnp.mean(hidden, axis=-1, keepdims=True)
    spread = jnp.mean(center * center, axis=-1, keepdims=True)
    return (center * lax.rsqrt(spread + EPSILON)).astype(jnp.bfloat16)


def late_kernel(q_ref, k_ref, v_ref, r_ref, wo_ref, out_ref, ctx_ref):
    bias, _ = window_bias()
    for row0 in range(0, q_ref.shape[0], TILE):
        span = slice(row0, row0 + TILE + WINDOW)
        attend(q_ref, k_ref[span, :], v_ref[span, :], ctx_ref, row0, bias)
    out_ref[...] = finish_rows(ctx_ref, r_ref, wo_ref)


def block_for(lang_ref, owner, rank, lang_grp):
    block, local, seen = jnp.int32(0), jnp.int32(-1), jnp.int32(0)
    for b in range(lang_ref.shape[0]):
        lang = lang_ref[b]
        mine = lang // lang_grp == owner
        take = mine & (seen == rank)
        block = jnp.where(take, b, block)
        local = jnp.where(take, lang - owner * lang_grp, local)
        seen = seen + mine.astype(jnp.int32)
    return block, local


def early_kernel(
    groups, lang_grp, lang_ref, q_ref, rim_ref, k_ref, v_ref, r_ref, wo_ref, late_ref, *rest
):
    outs, (ctx_ref, kk_ref, vv_ref, rows_ref) = rest[:groups], rest[groups:]
    rows = q_ref.shape[0]
    width = q_ref.shape[1]
    kk_ref[:WINDOW, :] = rim_ref[:, :width]
    vv_ref[:WINDOW, :] = rim_ref[:, width:]
    kk_ref[WINDOW:, :] = k_ref[...]
    vv_ref[WINDOW:, :] = v_ref[...]
    bias, col = window_bias()
    first = lax.axis_index("seq") == 0
    for row0 in range(0, rows, TILE):
        span = slice(row0, row0 + TILE + WINDOW)
        shut = jnp.logical_and(first, col + row0 < WINDOW)
        attend(q_ref, kk_ref[span, :], vv_ref[span, :], ctx_ref, row0, jnp.where(shut, NEG, bias))
    blocks = lang_ref.shape[0]
    length = rows_ref.shape[1]
    done = finish_rows(ctx_ref, r_ref, wo_ref)
    split = rows // length
    rows_ref[:split] = done.reshape(split, length, -1)
    rows_ref[split:] = late_ref[...].reshape(blocks - split, length, -1)
    me = lax.axis_index("grp")
    for step, out_ref in enumerate(outs):
        owner = peer_of(me, step, groups)
        for j in range(out_ref.shape[0] // length):
            block, _ = block_for(lang_ref, owner, j, lang_grp)
            out_ref[j * length : (j + 1) * length, :] = rows_ref[block]


def pack_kernel(groups, lang_grp, lang_ref, c_ref, *outs):
    length = c_ref.shape[1]
    me = lax.axis_index("grp")
    for step, out_ref in enumerate(outs):
        owner = peer_of(me, step, groups)
        cap = (out_ref.shape[0] - MARK) // length
        row = lax.broadcasted_iota(jnp.int32, (MARK, out_ref.shape[1]), 0)
        mark = jnp.full(row.shape, -1.0, jnp.float32)
        for j in range(cap):
            block, local = block_for(lang_ref, owner, j, lang_grp)
            out_ref[j * length : (j + 1) * length, :] = c_ref[block]
            mark = jnp.where(row == j, local.astype(jnp.float32), mark)
        out_ref[cap * length :, :] = mark.astype(jnp.bfloat16)


def gelu_slope(v):
    rate = math.sqrt(2 / math.pi)
    square = v * v
    t = jnp.tanh(rate * v * (1.0 + 0.044715 * square))
    return 0.5 * (1.0 + t) + (0.5 * rate) * v * (1.0 - t * t) * (1.0 + (3 * 0.044715) * square)


def project(x, cot, downs, ups, marks, length, lang_grp):
    pre, back = [], []
    for l in range(lang_grp):
        w_down = jnp.concatenate([d[l] for d in downs], axis=0)
        w_up = jnp.concatenate([u[l] for u in ups], axis=1)
        pre.append(dot(x, w_down, ((1,), (0,))))
        back.append(dot(cot, w_up, ((1,), (1,))))
    for j, lang in enumerate(marks):
        span = slice(j * length, (j + 1) * length)
        value, other = pre[0][span], back[0][span]
        for l in range(1, lang_grp):
            value = jnp.where(lang == l, pre[l][span], value)
            other = jnp.where(lang == l, back[l][span], other)
        yield span, value, other


def block_marks(cots, length, units):
    found = []
    for ref in cots:
        part = ref.shape[0] - MARK
        rows = ref[part:, :units].astype(jnp.float32)
        found += [rows[j : j + 1, :] for j in range(part // length)]
    return found


def by_offset(refs, offsets, size, width, to_ref):
    place = ring_place(lax.axis_index("seq"), size)
    part = to_ref.shape[0] // len(refs)
    for at, k in enumerate(offsets):
        member = ring_member((place + k) % size, size)
        columns = pl.ds(pl.multiple_of(member * width, width), width)
        for i, ref in enumerate(refs):
            to_ref[i * part : (i + 1) * part, at * width : (at + 1) * width] = ref[:part, columns]


def first_kernel(groups, near, far, size, length, *refs):
    refs = list(refs)
    take = lambda count: [refs.pop(0) for _ in range(count)]
    rows, cots = take(groups), take(groups)
    chunks = max(1, len(near))
    downs, ups = take(chunks), take(chunks)
    x_ref, pre_ref, back_ref, c_ref = refs
    lang_grp, width, units = downs[0].shape
    if near:
        by_offset(rows, near + far, size, width, x_ref)
        by_offset(cots, near, size, width, c_ref)
    else:
        part = rows[0].shape[0]
        for i in range(groups):
            x_ref[i * part : (i + 1) * part, :] = rows[i][...]
            c_ref[i * part : (i + 1) * part, :] = cots[i][:part, :]
    marks = block_marks(cots, length, units)
    x = x_ref[:, : c_ref.shape[1]]
    for span, value, other in project(x, c_ref[...], downs, ups, marks, length, lang_grp):
        pre_ref[span, :] = value
        back_ref[span, :] = other


def gate_kernel(groups, near, far, size, length, inv_scale, *refs):
    refs = list(refs)
    take = lambda count: [refs.pop(0) for _ in range(count)]
    x_ref, pre_ref, back_ref, bias_ref = take(4)
    cots, downs, ups = take(groups), take(len(far)), take(len(far))
    g_ref = refs.pop(0)
    lang_grp, units = bias_ref.shape
    marks = block_marks(cots, length, units)
    if far:
        c_ref = refs.pop()
        width = downs[0].shape[1]
        by_offset(cots, far, size, width, c_ref)
        at = len(near) * width
        x = x_ref[:, at : at + len(far) * width]
        terms = project(x, c_ref[...], downs, ups, marks, length, lang_grp)
    else:
        terms = ((slice(j * length, (j + 1) * length), 0.0, 0.0) for j in range(len(marks)))
    for (span, value, other), lang in zip(terms, marks):
        bias = jnp.zeros((1, units), jnp.float32)
        for l in range(lang_grp):
            bias = jnp.where(lang == l, bias_ref[l : l + 1, :].astype(jnp.float32), bias)
        gate = gelu_slope(pre_ref[span, :] + value + bias) * (back_ref[span, :] + other)
        gate = gate.astype(jnp.bfloat16)
        for l in range(lang_grp):
            g_ref[span, l * units : (l + 1) * units] = jnp.where(
                lang == l, gate, jnp.zeros_like(gate)
            )
    slabs(x_ref, g_ref, refs, len(near), inv_scale)


def slabs(x_ref, g_ref, outs, skip, inv_scale):
    at = skip * 2 * outs[0].shape[0] if outs else 0
    for out_ref in outs:
        count = out_ref.shape[0]
        slab = dot(x_ref[:, at : at + count], g_ref[...], ((0,), (0,)))
        out_ref[...] = (slab * inv_scale).astype(out_ref.dtype)
        at += count


def slab_kernel(inv_scale, x_ref, g_ref, *outs):
    slabs(x_ref, g_ref, outs, 0, inv_scale)


def cycle_gather(value, size, far):
    held = {0: value}
    half = size // 2
    for way in (-1, 1):
        moving = value
        for hop in range(1, half + (1 if way == far else 0)):
            moving = lax.ppermute(moving, "seq", ring_pairs(size, -way))
            held[(way * hop) % size] = moving
    return [held[k] for k in range(size)]


def cycle_reduce(parts, size, far):
    half = size // 2
    total = parts[0].astype(jnp.float32)
    for way in (1, -1):
        hops = half if way == far else half - 1
        moving = parts[(way * hops) % size]
        for hop in range(hops - 1, -1, -1):
            moving = lax.ppermute(moving, "seq", ring_pairs(size, way))
            if hop:
                mine = parts[(way * hop) % size]
                moving = (moving.astype(jnp.float32) + mine.astype(jnp.float32)).astype(mine.dtype)
        total = total + moving.astype(jnp.float32)
    return total


def kernel(fn, **options):
    return pl.pallas_call(fn, **options)


def body(queries, keys, values, resid, w_out, block_lang, w_down, w_up, bias_down, cotangent):
    tok_dev, width_q = queries.shape
    model = resid.shape[1]
    blocks = block_lang.shape[0]
    length = tok_dev // blocks
    groups = lax.axis_size("grp")
    size = lax.axis_size("seq")
    cap = max(1, blocks // groups)
    lang_grp, _, units = w_down.shape
    bf16 = jnp.bfloat16
    late = tok_dev - WINDOW

    edge = jnp.concatenate([keys[late:], values[late:]], axis=1)
    rim = lax.ppermute(edge, "seq", [(i, i + 1) for i in range(size - 1)])

    downs = cycle_gather(w_down, size, -1)
    ups = cycle_gather(w_up, size, 1)

    cot_out = kernel(
        functools.partial(pack_kernel, groups, lang_grp),
        out_shape=[jax.ShapeDtypeStruct((cap * length + MARK, model), bf16)] * groups,
        in_specs=[SMEM, VMEM],
        out_specs=[VMEM] * groups,
    )(block_lang, cotangent.reshape(blocks, length, model))

    def exchange(messages):
        got = [messages[0]]
        for step in range(1, groups):
            pairs = [(i, peer_of(i, step, groups)) for i in range(groups)]
            got.append(lax.ppermute(messages[step], "grp", pairs))
        return got

    cots = exchange(cot_out)

    def block_spec(shape, index):
        return pl.BlockSpec(shape, lambda i: index)

    full = lambda a: block_spec(a.shape, (0,) * a.ndim)
    half_q = late // WINDOW
    rows_late = kernel(
        late_kernel,
        grid=(1,),
        out_shape=jax.ShapeDtypeStruct((late, model), bf16),
        in_specs=[
            block_spec((late, width_q), (half_q, 0)),
            full(keys),
            full(values),
            block_spec((late, model), (half_q, 0)),
            full(w_out),
        ],
        out_specs=block_spec((late, model), (0, 0)),
        scratch_shapes=[pltpu.VMEM((late, width_q), bf16)],
    )(queries, keys, values, resid, w_out)

    row_out = kernel(
        functools.partial(early_kernel, groups, lang_grp),
        grid=(1,),
        out_shape=[jax.ShapeDtypeStruct((cap * length, model), bf16)] * groups,
        in_specs=[
            SMEM,
            block_spec((WINDOW, width_q), (0, 0)),
            full(rim),
            block_spec((WINDOW, width_q), (0, 0)),
            block_spec((WINDOW, width_q), (0, 0)),
            block_spec((WINDOW, model), (0, 0)),
            full(w_out),
            full(rows_late),
        ],
        out_specs=[block_spec((cap * length, model), (0, 0))] * groups,
        scratch_shapes=[
            pltpu.VMEM((WINDOW, width_q), bf16),
            pltpu.VMEM((2 * WINDOW, width_q), bf16),
            pltpu.VMEM((2 * WINDOW, width_q), bf16),
            pltpu.VMEM((blocks, length, model), bf16),
        ],
    )(block_lang, queries, rim, keys, values, resid, w_out, rows_late)
    rows = exchange(row_out)

    share = model // size
    whole = share % LANES != 0
    cells = lang_grp * units
    half = size // 2
    near, far = [], []
    if whole:
        place = ring_place(lax.axis_index("seq"), size)
        at_offset = ring_member((place + jnp.arange(size)) % size, size)
        of_member = jnp.argsort(at_offset)
        stack = jnp.take(jnp.stack(downs), of_member, axis=0)
        downs = [stack.transpose(1, 0, 2, 3).reshape(lang_grp, model, units)]
        stack = jnp.take(jnp.stack(ups), of_member, axis=0)
        ups = [stack.transpose(1, 2, 0, 3).reshape(lang_grp, units, model)]
        downs_near, ups_near, downs_far, ups_far = downs, ups, [], []
        far_rows, near_rows = [], [model]
        near_width = model
    else:
        far = [half, half - 1, half + 1]
        near = [k for k in range(size) if k not in far]
        pick = lambda held, offsets: [held[k] for k in offsets]
        downs_near, ups_near = pick(downs, near), pick(ups, near)
        downs_far, ups_far = pick(downs, far), pick(ups, far)
        far_rows, near_rows = [share // 2] * (2 * len(far)), [share // 2] * (2 * len(near))
        near_width = share * len(near)
    tokens = groups * cap * length
    struct = jax.ShapeDtypeStruct
    x_all, pre, back = kernel(
        functools.partial(first_kernel, groups, near, far, size, length),
        out_shape=[
            struct((tokens, model), bf16),
            struct((tokens, units), jnp.float32),
            struct((tokens, units), jnp.float32),
        ],
        in_specs=[VMEM] * (2 * groups + 2 * len(downs_near)),
        out_specs=[VMEM] * 3,
        scratch_shapes=[pltpu.VMEM((tokens, near_width), bf16)],
    )(*rows, *cots, *downs_near, *ups_near)
    inv_scale = 1.0 / math.sqrt(tok_dev * size)
    gate, *far_slabs = kernel(
        functools.partial(gate_kernel, groups, near, far, size, length, inv_scale),
        out_shape=[struct((tokens, cells), bf16)] + [struct((c, cells), bf16) for c in far_rows],
        in_specs=[VMEM] * (4 + groups + 2 * len(far)),
        out_specs=[VMEM] * (1 + len(far_rows)),
        scratch_shapes=[pltpu.VMEM((tokens, share * len(far)), bf16)] if far else [],
    )(x_all, pre, back, bias_down, *cots, *downs_far, *ups_far)
    near_slabs = kernel(
        functools.partial(slab_kernel, inv_scale),
        out_shape=[struct((c, cells), bf16) for c in near_rows],
        in_specs=[VMEM] * 2,
        out_specs=[VMEM] * len(near_rows),
    )(x_all, gate)
    if whole:
        cut = jnp.take(near_slabs[0].reshape(size, 2, share // 2, cells), at_offset, axis=0)
        parts = [[cut[k, h] for k in range(size)] for h in range(2)]
    else:
        parts = []
        for h in range(2):
            found = dict(zip(near, near_slabs[h::2])) | dict(zip(far, far_slabs[h::2]))
            parts.append([found[k] for k in range(size)])
    upper = cycle_reduce(parts[0], size, 1)
    lower = cycle_reduce(parts[1], size, -1)
    return jnp.concatenate([upper, lower], axis=0).reshape(share, lang_grp, units)


def solution(mesh):
    in_specs = (
        P(("grp", "seq"), None),
        P(("grp", "seq"), None),
        P(("grp", "seq"), None),
        P(("grp", "seq"), None),
        P(),
        P(("grp", "seq")),
        P("grp", "seq", None),
        P("grp", None, "seq"),
        P("grp", None),
        P(("grp", "seq"), None),
    )
    out_specs = P("seq", "grp", None)

    return jax.shard_map(body, mesh=mesh, in_specs=in_specs, out_specs=out_specs, check_vma=False)
```

```python
import functools
import math

import jax
import jax.numpy as jnp
from jax import lax
from jax.experimental import pallas as pl
from jax.experimental.pallas import tpu as pltpu
from jax.sharding import PartitionSpec as P


HD = 64
WINDOW = 256
EPSILON = 1e-05
TILE = 128
LANES = 128
MARK = 16
NEG = -1e30
GRANT = 24 * 2**20


VMEM = pl.BlockSpec(memory_space=pltpu.VMEM)
SMEM = pl.BlockSpec(memory_space=pltpu.SMEM)


def ring_order(size):
    return list(range(0, size, 2)) + [i for i in range(size - 1, 0, -1) if i % 2]


def ring_pairs(size, step):
    order = ring_order(size)
    return [(order[i], order[(i + step) % size]) for i in range(size)]


def ring_place(index, size):
    half = index // 2
    return jnp.where(index % 2 == 0, half, size - 1 - half)


def ring_member(place, size):
    place = jnp.where(place >= size, place - size, place)
    ups = (size + 1) // 2
    return jnp.where(place < ups, 2 * place, 2 * (size - place) - 1)


def peer_of(index, step, size):
    if size & (size - 1) == 0:
        return index ^ step
    return (index + step) % size


def dot(a, b, dims):
    return lax.dot_general(a, b, (dims, ((), ())), preferred_element_type=jnp.float32)


def attend(q_ref, q_row, k_win, v_win, ctx_ref, row0, bias):
    width = q_ref.shape[1]
    group = min(width, 256)
    heads = group // HD
    for col0 in range(0, width, group):
        q_part = q_ref[q_row : q_row + TILE, col0 : col0 + group] * jnp.bfloat16(HD**-0.5)
        lane_head = lax.broadcasted_iota(jnp.int32, q_part.shape, 1) // HD
        q_diag = jnp.concatenate(
            [jnp.where(lane_head == h, q_part, jnp.zeros_like(q_part)) for h in range(heads)], axis=0
        )
        keys = k_win[:, col0 : col0 + group]
        vals = v_win[:, col0 : col0 + group]
        scores = dot(q_diag, keys, ((1,), (1,)))
        scores = scores.reshape(heads, TILE, scores.shape[1]) + bias[None]
        weights = jnp.exp(scores - jnp.max(scores, axis=-1, keepdims=True))
        inverse = 1.0 / jnp.sum(weights, axis=-1, keepdims=True)
        weights = weights.astype(jnp.bfloat16).reshape(heads * TILE, -1)
        mixed = dot(weights, vals, ((1,), (0,)))
        picked = jnp.zeros((TILE, group), jnp.float32)
        for h in range(heads):
            one = mixed[h * TILE : (h + 1) * TILE] * inverse[h]
            picked = jnp.where(lane_head == h, one, picked)
        ctx_ref[row0 : row0 + TILE, col0 : col0 + group] = picked.astype(jnp.bfloat16)


def window_bias():
    shape = (TILE, TILE + WINDOW)
    row = lax.broadcasted_iota(jnp.int32, shape, 0)
    col = lax.broadcasted_iota(jnp.int32, shape, 1)
    allowed = (col <= row + WINDOW) & (col > row)
    return jnp.where(allowed, 0.0, NEG).astype(jnp.float32), col


def finish_rows(ctx_ref, resid, wo_ref):
    hidden = (
        resid.astype(jnp.float32) + dot(ctx_ref[...], wo_ref[...], ((1,), (0,)))
    ).astype(jnp.bfloat16).astype(jnp.float32)
    center = hidden - jnp.mean(hidden, axis=-1, keepdims=True)
    spread = jnp.mean(center * center, axis=-1, keepdims=True)
    return (center * lax.rsqrt(spread + EPSILON)).astype(jnp.bfloat16)


def late_kernel(q_ref, k_ref, v_ref, r_ref, wo_ref, out_ref, ctx_ref):
    bias, _ = window_bias()
    for row0 in range(0, ctx_ref.shape[0], TILE):
        span = slice(row0, row0 + TILE + WINDOW)
        attend(q_ref, WINDOW + row0, k_ref[span, :], v_ref[span, :], ctx_ref, row0, bias)
    out_ref[...] = finish_rows(ctx_ref, r_ref[WINDOW:, :], wo_ref)


def block_for(lang_ref, owner, rank, lang_grp):
    block, local, seen = jnp.int32(0), jnp.int32(-1), jnp.int32(0)
    for b in range(lang_ref.shape[0]):
        lang = lang_ref[b]
        mine = (lang >= owner * lang_grp) & (lang < (owner + 1) * lang_grp)
        take = mine & (seen == rank)
        block = jnp.where(take, b, block)
        local = jnp.where(take, lang - owner * lang_grp, local)
        seen = seen + mine.astype(jnp.int32)
    return block, local


def early_kernel(
    groups, lang_grp, lang_ref, q_ref, rim_ref, k_ref, v_ref, r_ref, wo_ref, late_ref, *rest
):
    outs, (ctx_ref, kk_ref, vv_ref, rows_ref) = rest[:groups], rest[groups:]
    rows = WINDOW
    width = q_ref.shape[1]
    kk_ref[:WINDOW, :] = rim_ref[:, :width]
    vv_ref[:WINDOW, :] = rim_ref[:, width:]
    kk_ref[WINDOW:, :] = k_ref[:WINDOW, :]
    vv_ref[WINDOW:, :] = v_ref[:WINDOW, :]
    bias, col = window_bias()
    first = lax.axis_index("seq") == 0
    for row0 in range(0, rows, TILE):
        span = slice(row0, row0 + TILE + WINDOW)
        shut = jnp.logical_and(first, col + row0 < WINDOW)
        mask = jnp.where(shut, NEG, bias)
        attend(q_ref, row0, kk_ref[span, :], vv_ref[span, :], ctx_ref, row0, mask)
    blocks = lang_ref.shape[0]
    length = rows_ref.shape[1]
    done = finish_rows(ctx_ref, r_ref[:rows, :], wo_ref)
    split = rows // length
    rows_ref[:split] = done.reshape(split, length, -1)
    rows_ref[split:] = late_ref[...].reshape(blocks - split, length, -1)
    me = lax.axis_index("grp")
    for step, out_ref in enumerate(outs):
        owner = peer_of(me, step, groups)
        for j in range(out_ref.shape[0] // length):
            block, _ = block_for(lang_ref, owner, j, lang_grp)
            out_ref[j * length : (j + 1) * length, :] = rows_ref[block]


def pack_kernel(groups, lang_grp, lang_ref, c_ref, *outs):
    length = c_ref.shape[1]
    me = lax.axis_index("grp")
    for step, out_ref in enumerate(outs):
        owner = peer_of(me, step, groups)
        cap = (out_ref.shape[0] - MARK) // length
        row = lax.broadcasted_iota(jnp.int32, (MARK, out_ref.shape[1]), 0)
        mark = jnp.full(row.shape, -1.0, jnp.float32)
        for j in range(cap):
            block, local = block_for(lang_ref, owner, j, lang_grp)
            out_ref[j * length : (j + 1) * length, :] = c_ref[block]
            mark = jnp.where(row == j, local.astype(jnp.float32), mark)
        out_ref[cap * length :, :] = mark.astype(jnp.bfloat16)


def gelu_slope(v):
    rate = math.sqrt(2 / math.pi)
    square = v * v
    t = jnp.tanh(rate * v * (1.0 + 0.044715 * square))
    return 0.5 * (1.0 + t) + (0.5 * rate) * v * (1.0 - t * t) * (1.0 + (3 * 0.044715) * square)


def project(x, cot, downs, ups):
    lang_grp, width, units = downs[0].shape
    w_down = jnp.concatenate(
        [jnp.concatenate([d[l] for l in range(lang_grp)], axis=1) for d in downs], axis=0
    )
    w_up = jnp.concatenate([u[...].reshape(lang_grp * units, width) for u in ups], axis=1)
    return dot(x, w_down, ((1,), (0,))), dot(cot, w_up, ((1,), (1,)))


def of_language(table, lang, units):
    value = table[:, :units]
    for l in range(1, table.shape[1] // units):
        value = jnp.where(lang == l, table[:, l * units : (l + 1) * units], value)
    return value


def by_offset(refs, offsets, size, width, to_ref):
    place = ring_place(lax.axis_index("seq"), size)
    part = to_ref.shape[0] // len(refs)
    for at, k in enumerate(offsets):
        member = ring_member(place + k, size)
        columns = pl.ds(pl.multiple_of(member * width, width), width)
        for i, ref in enumerate(refs):
            to_ref[i * part : (i + 1) * part, at * width : (at + 1) * width] = ref[:part, columns]


def first_kernel(groups, near, far, size, length, *refs):
    refs = list(refs)
    take = lambda count: [refs.pop(0) for _ in range(count)]
    rows, cots = take(groups), take(groups)
    chunks = max(1, len(near))
    downs, ups = take(chunks), take(chunks)
    (bias_ref,) = take(1)
    turned_ref, pre_ref, back_ref, mark_ref = take(4)
    lang_grp, width, units = downs[0].shape
    part = rows[0].shape[0]
    if near:
        xf_ref, cf_ref, x_ref, c_ref = refs
        by_offset(rows, near, size, width, x_ref)
        by_offset(rows, far, size, width, xf_ref)
        by_offset(cots, near, size, width, c_ref)
        by_offset(cots, far, size, width, cf_ref)
        turned_ref[x_ref.shape[1] :, :] = xf_ref[...].T
    else:
        x_ref, c_ref = refs
        for i in range(groups):
            x_ref[i * part : (i + 1) * part, :] = rows[i][...]
            c_ref[i * part : (i + 1) * part, :] = cots[i][:part, :]
    turned_ref[: x_ref.shape[1], :] = x_ref[...].T
    pre, back = project(x_ref[...], c_ref[...], downs, ups)
    cap = part // length
    for i, ref in enumerate(cots):
        for j in range(cap):
            at = i * cap + j
            lang = ref[part:, :units].astype(jnp.float32)[j : j + 1, :]
            mark_ref[at : at + 1, :] = lang
            bias = bias_ref[0:1, :]
            for l in range(1, lang_grp):
                bias = jnp.where(lang == l, bias_ref[l : l + 1, :], bias)
            span = slice(at * length, (at + 1) * length)
            pre_ref[span, :] = of_language(pre[span], lang, units) + bias
            back_ref[span, :] = of_language(back[span], lang, units)


def gate_kernel(near, far, length, inv_scale, *refs):
    refs = list(refs)
    take = lambda count: [refs.pop(0) for _ in range(count)]
    turned_ref, pre_ref, back_ref, mark_ref = take(4)
    tokens, units = pre_ref.shape
    if far:
        xf_ref, cf_ref = take(2)
        downs, ups = take(len(far)), take(len(far))
        pre, back = project(xf_ref[...], cf_ref[...], downs, ups)
    g_ref = refs.pop(0)
    for j in range(tokens // length):
        span = slice(j * length, (j + 1) * length)
        lang = mark_ref[j : j + 1, :]
        value, other = pre_ref[span, :], back_ref[span, :]
        if far:
            value = value + of_language(pre[span], lang, units)
            other = other + of_language(back[span], lang, units)
        gate = (gelu_slope(value) * other).astype(jnp.bfloat16)
        for l in range(g_ref.shape[1] // units):
            g_ref[span, l * units : (l + 1) * units] = jnp.where(
                lang == l, gate, jnp.zeros_like(gate)
            )
    if far:
        slabs(turned_ref, len(near), g_ref, refs, inv_scale)


def slabs(turned_ref, skip, g_ref, outs, inv_scale):
    count = outs[0].shape[0]
    for i in range(0, len(outs), 2):
        at = (2 * skip + i) * count
        pair = outs[i : i + 2]
        slab = dot(turned_ref[at : at + len(pair) * count, :], g_ref[...], ((1,), (0,)))
        slab = (slab * inv_scale).astype(jnp.bfloat16)
        for h, out_ref in enumerate(pair):
            out_ref[...] = slab[h * count : (h + 1) * count]


def slab_kernel(inv_scale, turned_ref, g_ref, *outs):
    slabs(turned_ref, 0, g_ref, outs, inv_scale)


def close_kernel(*refs):
    out_ref = refs[-1]
    lang_grp, share, units = out_ref.shape
    count = share // 2
    for h in range(2):
        terms = [ref[...].astype(jnp.float32) for ref in refs[3 * h : 3 * h + 3]]
        total = terms[0] + terms[1] + terms[2]
        for l in range(lang_grp):
            out_ref[l, h * count : (h + 1) * count, :] = total[:, l * units : (l + 1) * units]


def cycle_gather(value, size, far):
    held = {0: value}
    half = size // 2
    for way in (-1, 1):
        moving = value
        for hop in range(1, half + (1 if way == far else 0)):
            moving = lax.ppermute(moving, "seq", ring_pairs(size, -way))
            held[(way * hop) % size] = moving
    return [held[k] for k in range(size)]


def cycle_reduce(parts, size, far):
    half = size // 2
    found = [parts[0]]
    for way in (1, -1):
        hops = half if way == far else half - 1
        moving = parts[(way * hops) % size]
        for hop in range(hops - 1, -1, -1):
            moving = lax.ppermute(moving, "seq", ring_pairs(size, way))
            if hop:
                mine = parts[(way * hop) % size]
                moving = (moving.astype(jnp.float32) + mine.astype(jnp.float32)).astype(mine.dtype)
        found.append(moving)
    return found


def kernel(fn, args, outs, scratch=(), final=False):
    small = [a.dtype == jnp.int32 for a in args]
    placed = [
        a if s else pltpu.with_memory_space_constraint(a, pltpu.VMEM) for a, s in zip(args, small)
    ]
    make = jax.ShapeDtypeStruct if final else pltpu.VMEM
    return pl.pallas_call(
        fn,
        out_shape=[make(shape, dtype) for shape, dtype in outs],
        in_specs=[SMEM if s else VMEM for s in small],
        out_specs=[VMEM] * len(outs),
        scratch_shapes=[pltpu.VMEM(shape, dtype) for shape, dtype in scratch],
        compiler_params=pltpu.CompilerParams(vmem_limit_bytes=GRANT),
    )(*placed)


def body(queries, keys, values, resid, w_out, block_lang, w_down, w_up, bias_down, cotangent):
    tok_dev, width_q = queries.shape
    model = resid.shape[1]
    blocks = block_lang.shape[0]
    length = tok_dev // blocks
    groups = lax.axis_size("grp")
    size = lax.axis_size("seq")
    cap = max(1, blocks // groups)
    lang_grp, _, units = w_down.shape
    bf16 = jnp.bfloat16
    late = tok_dev - WINDOW

    edge = jnp.concatenate([keys[late:], values[late:]], axis=1)
    rim = lax.ppermute(edge, "seq", [(i, i + 1) for i in range(size - 1)])

    downs = cycle_gather(w_down, size, -1)
    ups = cycle_gather(w_up, size, 1)

    cot_out = kernel(
        functools.partial(pack_kernel, groups, lang_grp),
        [block_lang, cotangent.reshape(blocks, length, model)],
        [((cap * length + MARK, model), bf16)] * groups,
    )

    def exchange(messages):
        got = [messages[0]]
        for step in range(1, groups):
            pairs = [(i, peer_of(i, step, groups)) for i in range(groups)]
            got.append(lax.ppermute(messages[step], "grp", pairs))
        return got

    cots = exchange(cot_out)

    (rows_late,) = kernel(
        late_kernel,
        [queries, keys, values, resid, w_out],
        [((late, model), bf16)],
        [((late, width_q), bf16)],
    )
    row_out = kernel(
        functools.partial(early_kernel, groups, lang_grp),
        [block_lang, queries, rim, keys, values, resid, w_out, rows_late],
        [((cap * length, model), bf16)] * groups,
        [
            ((WINDOW, width_q), bf16),
            ((2 * WINDOW, width_q), bf16),
            ((2 * WINDOW, width_q), bf16),
            ((blocks, length, model), bf16),
        ],
    )
    rows = exchange(row_out)

    share = model // size
    whole = share % LANES != 0
    cells = lang_grp * units
    half = size // 2
    near, far = [], []
    if whole:
        place = ring_place(lax.axis_index("seq"), size)
        at_offset = ring_member(place + jnp.arange(size), size)
        of_member = jnp.argsort(at_offset)
        stack = jnp.take(jnp.stack(downs), of_member, axis=0)
        downs = [stack.transpose(1, 0, 2, 3).reshape(lang_grp, model, units)]
        stack = jnp.take(jnp.stack(ups), of_member, axis=0)
        ups = [stack.transpose(1, 2, 0, 3).reshape(lang_grp, units, model)]
        downs_near, ups_near, downs_far, ups_far = downs, ups, [], []
        far_rows, near_rows = [], [model]
        near_width = model
    else:
        far = [half, half - 1, half + 1]
        near = [k for k in range(size) if k not in far]
        pick = lambda held, offsets: [held[k] for k in offsets]
        downs_near, ups_near = pick(downs, near), pick(ups, near)
        downs_far, ups_far = pick(downs, far), pick(ups, far)
        far_rows, near_rows = [share // 2] * (2 * len(far)), [share // 2] * (2 * len(near))
        near_width = share * len(near)
    tokens = groups * cap * length
    far_width = share * len(far)
    f32 = jnp.float32
    spare = [((tokens, far_width), bf16)] * 2 if far else []
    turned, pre, back, marks, *far_x = kernel(
        functools.partial(first_kernel, groups, near, far, size, length),
        [*rows, *cots, *downs_near, *ups_near, bias_down.astype(f32)],
        [
            ((model, tokens), bf16),
            ((tokens, units), f32),
            ((tokens, units), f32),
            ((tokens // length, units), f32),
        ]
        + spare,
        [((tokens, near_width), bf16)] * 2,
    )
    inv_scale = 1.0 / math.sqrt(tok_dev * size)
    gate, *far_slabs = kernel(
        functools.partial(gate_kernel, near, far, length, inv_scale),
        [turned, pre, back, marks, *far_x, *downs_far, *ups_far],
        [((tokens, cells), bf16)] + [((c, cells), bf16) for c in far_rows],
    )
    near_slabs = kernel(
        functools.partial(slab_kernel, inv_scale),
        [turned, gate],
        [((c, cells), bf16) for c in near_rows],
    )
    if whole:
        cut = jnp.take(near_slabs[0].reshape(size, 2, share // 2, cells), at_offset, axis=0)
        parts = [[cut[k, h] for k in range(size)] for h in range(2)]
    else:
        parts = []
        for h in range(2):
            found = dict(zip(near, near_slabs[h::2])) | dict(zip(far, far_slabs[h::2]))
            parts.append([found[k] for k in range(size)])
    upper = cycle_reduce(parts[0], size, 1)
    lower = cycle_reduce(parts[1], size, -1)
    (total,) = kernel(close_kernel, [*upper, *lower], [((lang_grp, share, units), f32)], final=True)
    return total.transpose(1, 0, 2)


def solution(mesh):
    in_specs = (
        P(("grp", "seq"), None),
        P(("grp", "seq"), None),
        P(("grp", "seq"), None),
        P(("grp", "seq"), None),
        P(),
        P(("grp", "seq")),
        P("grp", "seq", None),
        P("grp", None, "seq"),
        P("grp", None),
        P(("grp", "seq"), None),
    )
    out_specs = P("seq", "grp", None)

    return jax.shard_map(body, mesh=mesh, in_specs=in_specs, out_specs=out_specs, check_vma=False)
```

```python
import functools
import math

import jax
import jax.numpy as jnp
from jax import lax
from jax.experimental import pallas as pl
from jax.experimental.pallas import tpu as pltpu
from jax.sharding import PartitionSpec as P


HD = 64
WINDOW = 256
EPSILON = 1e-05
TILE = 128
LANES = 128
MARK = 16
NEG = -1e30
GRANT = 24 * 2**20


VMEM = pl.BlockSpec(memory_space=pltpu.VMEM)
SMEM = pl.BlockSpec(memory_space=pltpu.SMEM)


def ring_order(size):
    return list(range(0, size, 2)) + [i for i in range(size - 1, 0, -1) if i % 2]


def ring_pairs(size, step):
    order = ring_order(size)
    return [(order[i], order[(i + step) % size]) for i in range(size)]


def ring_place(index, size):
    half = index // 2
    return jnp.where(index % 2 == 0, half, size - 1 - half)


def ring_member(place, size):
    place = jnp.where(place >= size, place - size, place)
    ups = (size + 1) // 2
    return jnp.where(place < ups, 2 * place, 2 * (size - place) - 1)


def peer_of(index, step, size):
    if size & (size - 1) == 0:
        return index ^ step
    return (index + step) % size


def dot(a, b, dims):
    return lax.dot_general(a, b, (dims, ((), ())), preferred_element_type=jnp.float32)


def attend(q_ref, q_row, k_win, v_win, ctx_ref, row0, bias):
    width = q_ref.shape[1]
    group = min(width, 256)
    heads = group // HD
    for col0 in range(0, width, group):
        q_part = q_ref[q_row : q_row + TILE, col0 : col0 + group] * jnp.bfloat16(HD**-0.5)
        lane_head = lax.broadcasted_iota(jnp.int32, q_part.shape, 1) // HD
        q_diag = jnp.concatenate(
            [jnp.where(lane_head == h, q_part, jnp.zeros_like(q_part)) for h in range(heads)], axis=0
        )
        keys = k_win[:, col0 : col0 + group]
        vals = v_win[:, col0 : col0 + group]
        scores = dot(q_diag, keys, ((1,), (1,)))
        scores = scores.reshape(heads, TILE, scores.shape[1]) + bias[None]
        weights = jnp.exp(scores - jnp.max(scores, axis=-1, keepdims=True))
        inverse = 1.0 / jnp.sum(weights, axis=-1, keepdims=True)
        weights = weights.astype(jnp.bfloat16).reshape(heads * TILE, -1)
        mixed = dot(weights, vals, ((1,), (0,)))
        picked = jnp.zeros((TILE, group), jnp.float32)
        for h in range(heads):
            one = mixed[h * TILE : (h + 1) * TILE] * inverse[h]
            picked = jnp.where(lane_head == h, one, picked)
        ctx_ref[row0 : row0 + TILE, col0 : col0 + group] = picked.astype(jnp.bfloat16)


def window_bias():
    shape = (TILE, TILE + WINDOW)
    row = lax.broadcasted_iota(jnp.int32, shape, 0)
    col = lax.broadcasted_iota(jnp.int32, shape, 1)
    allowed = (col <= row + WINDOW) & (col > row)
    return jnp.where(allowed, 0.0, NEG).astype(jnp.float32), col


def finish_rows(ctx_ref, resid, wo_ref):
    hidden = (
        resid.astype(jnp.float32) + dot(ctx_ref[...], wo_ref[...], ((1,), (0,)))
    ).astype(jnp.bfloat16).astype(jnp.float32)
    center = hidden - jnp.mean(hidden, axis=-1, keepdims=True)
    spread = jnp.mean(center * center, axis=-1, keepdims=True)
    return (center * lax.rsqrt(spread + EPSILON)).astype(jnp.bfloat16)


def late_kernel(q_ref, k_ref, v_ref, r_ref, wo_ref, out_ref, ctx_ref):
    bias, _ = window_bias()
    for row0 in range(0, ctx_ref.shape[0], TILE):
        span = slice(row0, row0 + TILE + WINDOW)
        attend(q_ref, WINDOW + row0, k_ref[span, :], v_ref[span, :], ctx_ref, row0, bias)
    out_ref[...] = finish_rows(ctx_ref, r_ref[WINDOW:, :], wo_ref)


def block_for(lang_ref, owner, rank, lang_grp):
    block, local, seen = jnp.int32(0), jnp.int32(-1), jnp.int32(0)
    for b in range(lang_ref.shape[0]):
        lang = lang_ref[b]
        mine = (lang >= owner * lang_grp) & (lang < (owner + 1) * lang_grp)
        take = mine & (seen == rank)
        block = jnp.where(take, b, block)
        local = jnp.where(take, lang - owner * lang_grp, local)
        seen = seen + mine.astype(jnp.int32)
    return block, local


def early_kernel(
    groups, lang_grp, lang_ref, q_ref, rim_ref, k_ref, v_ref, r_ref, wo_ref, late_ref, *rest
):
    outs, (ctx_ref, kk_ref, vv_ref, rows_ref) = rest[:groups], rest[groups:]
    rows = WINDOW
    width = q_ref.shape[1]
    kk_ref[:WINDOW, :] = rim_ref[:, :width]
    vv_ref[:WINDOW, :] = rim_ref[:, width:]
    kk_ref[WINDOW:, :] = k_ref[:WINDOW, :]
    vv_ref[WINDOW:, :] = v_ref[:WINDOW, :]
    bias, col = window_bias()
    first = lax.axis_index("seq") == 0
    for row0 in range(0, rows, TILE):
        span = slice(row0, row0 + TILE + WINDOW)
        shut = jnp.logical_and(first, col + row0 < WINDOW)
        mask = jnp.where(shut, NEG, bias)
        attend(q_ref, row0, kk_ref[span, :], vv_ref[span, :], ctx_ref, row0, mask)
    blocks = lang_ref.shape[0]
    length = rows_ref.shape[1]
    done = finish_rows(ctx_ref, r_ref[:rows, :], wo_ref)
    split = rows // length
    rows_ref[:split] = done.reshape(split, length, -1)
    rows_ref[split:] = late_ref[...].reshape(blocks - split, length, -1)
    me = lax.axis_index("grp")
    for step, out_ref in enumerate(outs):
        owner = peer_of(me, step, groups)
        for j in range(out_ref.shape[0] // length):
            block, _ = block_for(lang_ref, owner, j, lang_grp)
            out_ref[j * length : (j + 1) * length, :] = rows_ref[block]


def pack_kernel(groups, lang_grp, lang_ref, c_ref, *outs):
    length = c_ref.shape[1]
    me = lax.axis_index("grp")
    for step, out_ref in enumerate(outs):
        owner = peer_of(me, step, groups)
        cap = (out_ref.shape[0] - MARK) // length
        row = lax.broadcasted_iota(jnp.int32, (MARK, out_ref.shape[1]), 0)
        mark = jnp.full(row.shape, -1.0, jnp.float32)
        for j in range(cap):
            block, local = block_for(lang_ref, owner, j, lang_grp)
            out_ref[j * length : (j + 1) * length, :] = c_ref[block]
            mark = jnp.where(row == j, local.astype(jnp.float32), mark)
        out_ref[cap * length :, :] = mark.astype(jnp.bfloat16)


def gelu_slope(v):
    rate = math.sqrt(2 / math.pi)
    square = v * v
    t = jnp.tanh(rate * v * (1.0 + 0.044715 * square))
    return 0.5 * (1.0 + t) + (0.5 * rate) * v * (1.0 - t * t) * (1.0 + (3 * 0.044715) * square)


def lead_units(units):
    return max(1, round(2 * units / 3 / LANES)) * LANES if units > LANES else units


def by_offset(refs, offsets, size, width, to_ref):
    place = ring_place(lax.axis_index("seq"), size)
    part = to_ref.shape[0] // len(refs)
    for at, k in enumerate(offsets):
        member = ring_member(place + k, size)
        columns = pl.ds(pl.multiple_of(member * width, width), width)
        for i, ref in enumerate(refs):
            to_ref[i * part : (i + 1) * part, at * width : (at + 1) * width] = ref[:part, columns]


def lead_or_rest(units, first):
    return units - first if first else lead_units(units)


def lay_kernel(groups, offsets, length, *refs):
    rows, cots = refs[:groups], refs[groups : 2 * groups]
    x_ref, c_ref, turned_ref, mark_ref = refs[2 * groups :]
    part = rows[0].shape[0]
    if offsets:
        width = x_ref.shape[1] // len(offsets)
        by_offset(rows, offsets, len(offsets), width, x_ref)
        by_offset(cots, offsets, len(offsets), width, c_ref)
    else:
        for i in range(groups):
            x_ref[i * part : (i + 1) * part, :] = rows[i][...]
            c_ref[i * part : (i + 1) * part, :] = cots[i][:part, :]
    turned_ref[...] = x_ref[...].T
    cap = part // length
    for i, ref in enumerate(cots):
        marks = ref[part:, : mark_ref.shape[1]].astype(jnp.float32)
        mark_ref[i * cap : (i + 1) * cap, :] = marks[:cap, :]


def products(x, cot, downs, ups, first, units):
    lang_grp, _, _ = downs[0].shape
    chosen = slice(first, first + units)
    w_down = jnp.concatenate(
        [jnp.concatenate([d[l, :, chosen] for l in range(lang_grp)], axis=1) for d in downs], axis=0
    )
    w_up = jnp.concatenate(
        [jnp.concatenate([u[l, chosen, :] for l in range(lang_grp)], axis=0) for u in ups], axis=1
    )
    return dot(x, w_down, ((1,), (0,))), dot(cot, w_up, ((1,), (1,)))


def of_language(table, lang, units):
    value = table[:, :units]
    for l in range(1, table.shape[1] // units):
        value = jnp.where(lang == l, table[:, l * units : (l + 1) * units], value)
    return value


def near_kernel(chunks, length, x_ref, c_ref, mark_ref, bias_ref, *refs):
    downs, ups, (pre_ref, back_ref) = refs[:chunks], refs[chunks : 2 * chunks], refs[2 * chunks :]
    lang_grp, width, units = downs[0].shape
    reach = chunks * width
    pre, back = products(x_ref[:, :reach], c_ref[:, :reach], downs, ups, 0, units)
    for j in range(x_ref.shape[0] // length):
        span = slice(j * length, (j + 1) * length)
        lang = mark_ref[j : j + 1, :]
        bias = bias_ref[0:1, :].astype(jnp.float32)
        for l in range(1, lang_grp):
            bias = jnp.where(lang == l, bias_ref[l : l + 1, :].astype(jnp.float32), bias)
        pre_ref[span, :] = of_language(pre[span], lang, units) + bias
        back_ref[span, :] = of_language(back[span], lang, units)


def gate_kernel(chunks, length, skip, first, inv_scale, *refs):
    x_ref, c_ref, turned_ref, mark_ref, pre_ref, back_ref = refs[:6]
    downs, ups = refs[6 : 6 + chunks], refs[6 + chunks : 6 + 2 * chunks]
    g_ref, *outs = refs[6 + 2 * chunks :]
    units = lead_or_rest(pre_ref.shape[1], first)
    lang_grp = g_ref.shape[1] // units
    if chunks:
        at = x_ref.shape[1] - chunks * downs[0].shape[1]
        pre, back = products(x_ref[:, at:], c_ref[:, at:], downs, ups, first, units)
    chosen = slice(first, first + units)
    for j in range(pre_ref.shape[0] // length):
        span = slice(j * length, (j + 1) * length)
        lang = mark_ref[j : j + 1, :units]
        value, other = pre_ref[span, chosen], back_ref[span, chosen]
        if chunks:
            value = value + of_language(pre[span], lang, units)
            other = other + of_language(back[span], lang, units)
        gate = (gelu_slope(value) * other).astype(jnp.bfloat16)
        for l in range(lang_grp):
            g_ref[span, l * units : (l + 1) * units] = jnp.where(
                lang == l, gate, jnp.zeros_like(gate)
            )
    slabs(turned_ref, skip, g_ref, outs, inv_scale)


def slabs(turned_ref, skip, g_ref, outs, inv_scale):
    for i, out_ref in enumerate(outs):
        count = out_ref.shape[0]
        at = (skip + i) * count
        slab = dot(turned_ref[at : at + count, :], g_ref[...], ((1,), (0,)))
        out_ref[...] = (slab * inv_scale).astype(out_ref.dtype)


def slab_kernel(inv_scale, turned_ref, g_ref, *outs):
    slabs(turned_ref, 0, g_ref, outs, inv_scale)


def close_kernel(*refs):
    out_ref = refs[-1]
    lang_grp = out_ref.shape[0]
    first = 0
    for at in range(0, len(refs) - 1, 3):
        terms = [ref[...].astype(jnp.float32) for ref in refs[at : at + 3]]
        total = terms[0] + terms[1] + terms[2]
        units = total.shape[1] // lang_grp
        for l in range(lang_grp):
            out_ref[l, :, first : first + units] = total[:, l * units : (l + 1) * units]
        first += units


def cycle_gather(value, size, far):
    held = {0: value}
    half = size // 2
    for way in (-1, 1):
        moving = value
        for hop in range(1, half + (1 if way == far else 0)):
            moving = lax.ppermute(moving, "seq", ring_pairs(size, -way))
            held[(way * hop) % size] = moving
    return [held[k] for k in range(size)]


def cycle_reduce(parts, size, far):
    half = size // 2
    found = [parts[0]]
    for way in (1, -1):
        hops = half if way == far else half - 1
        moving = parts[(way * hops) % size]
        for hop in range(hops - 1, -1, -1):
            moving = lax.ppermute(moving, "seq", ring_pairs(size, way))
            if hop:
                mine = parts[(way * hop) % size]
                wide = moving.astype(jnp.float32) + mine.astype(jnp.float32)
                moving = wide.astype(mine.dtype)
        found.append(moving)
    return found


def kernel(fn, args, outs, scratch=(), final=False):
    small = [a.dtype == jnp.int32 for a in args]
    placed = [
        a if s else pltpu.with_memory_space_constraint(a, pltpu.VMEM) for a, s in zip(args, small)
    ]
    make = jax.ShapeDtypeStruct if final else pltpu.VMEM
    return pl.pallas_call(
        fn,
        out_shape=[make(shape, dtype) for shape, dtype in outs],
        in_specs=[SMEM if s else VMEM for s in small],
        out_specs=[VMEM] * len(outs),
        scratch_shapes=[pltpu.VMEM(shape, dtype) for shape, dtype in scratch],
        compiler_params=pltpu.CompilerParams(vmem_limit_bytes=GRANT),
    )(*placed)


def body(queries, keys, values, resid, w_out, block_lang, w_down, w_up, bias_down, cotangent):
    tok_dev, width_q = queries.shape
    model = resid.shape[1]
    blocks = block_lang.shape[0]
    length = tok_dev // blocks
    groups = lax.axis_size("grp")
    size = lax.axis_size("seq")
    cap = max(1, blocks // groups)
    lang_grp, _, units = w_down.shape
    bf16 = jnp.bfloat16
    late = tok_dev - WINDOW

    edge = jnp.concatenate([keys[late:], values[late:]], axis=1)
    rim = lax.ppermute(edge, "seq", [(i, i + 1) for i in range(size - 1)])

    downs = cycle_gather(w_down, size, -1)
    ups = cycle_gather(w_up, size, 1)

    cot_out = kernel(
        functools.partial(pack_kernel, groups, lang_grp),
        [block_lang, cotangent.reshape(blocks, length, model)],
        [((cap * length + MARK, model), bf16)] * groups,
    )

    def exchange(messages):
        got = [messages[0]]
        for step in range(1, groups):
            pairs = [(i, peer_of(i, step, groups)) for i in range(groups)]
            got.append(lax.ppermute(messages[step], "grp", pairs))
        return got

    cots = exchange(cot_out)

    (rows_late,) = kernel(
        late_kernel,
        [queries, keys, values, resid, w_out],
        [((late, model), bf16)],
        [((late, width_q), bf16)],
    )
    row_out = kernel(
        functools.partial(early_kernel, groups, lang_grp),
        [block_lang, queries, rim, keys, values, resid, w_out, rows_late],
        [((cap * length, model), bf16)] * groups,
        [
            ((WINDOW, width_q), bf16),
            ((2 * WINDOW, width_q), bf16),
            ((2 * WINDOW, width_q), bf16),
            ((blocks, length, model), bf16),
        ],
    )
    rows = exchange(row_out)

    share = w_down.shape[1]
    whole = share % LANES != 0
    half = size // 2
    if whole:
        place = ring_place(lax.axis_index("seq"), size)
        at_offset = ring_member(place + jnp.arange(size), size)
        of_member = jnp.argsort(at_offset)
        stack = jnp.take(jnp.stack(downs), of_member, axis=0)
        downs = [stack.transpose(1, 0, 2, 3).reshape(lang_grp, model, units)]
        stack = jnp.take(jnp.stack(ups), of_member, axis=0)
        ups = [stack.transpose(1, 2, 0, 3).reshape(lang_grp, units, model)]
        early_slabs, offsets, slab_rows, last = 0, [], [model], 0
    else:
        tops = [half + 1, half - 1, half]
        rest = [k for k in range(size) if k not in tops]
        offsets, slab_rows, last = rest + tops, [share] * len(rest), 1
        downs, ups = [downs[k] for k in offsets], [ups[k] for k in offsets]
        early_slabs = len(tops)
    tokens = groups * cap * length
    f32 = jnp.float32
    x_all, c_all, turned, marks = kernel(
        functools.partial(lay_kernel, groups, offsets, length),
        [*rows, *cots],
        [
            ((tokens, model), bf16),
            ((tokens, model), bf16),
            ((model, tokens), bf16),
            ((tokens // length, units), f32),
        ],
    )
    near = len(downs) - last
    pre, back = kernel(
        functools.partial(near_kernel, near, length),
        [x_all, c_all, marks, bias_down, *downs[:near], *ups[:near]],
        [((tokens, units), f32)] * 2,
    )
    inv_scale = 1.0 / math.sqrt(tok_dev * size)
    lead = lead_units(units)
    sums = []
    for first, way in ((0, 1), (lead, -1)):
        count = lead_or_rest(units, first)
        if not count:
            continue
        cells = lang_grp * count
        skip = len(offsets) - early_slabs
        gate, *top_slabs = kernel(
            functools.partial(gate_kernel, last, length, skip, first, inv_scale),
            [x_all, c_all, turned, marks, pre, back, *downs[near:], *ups[near:]],
            [((tokens, cells), bf16)] + [((share, cells), bf16)] * early_slabs,
        )
        rest_slabs = kernel(
            functools.partial(slab_kernel, inv_scale),
            [turned, gate],
            [((c, cells), bf16) for c in slab_rows],
        )
        if whole:
            cut = jnp.take(rest_slabs[0].reshape(size, share, cells), at_offset, axis=0)
            parts = [cut[k] for k in range(size)]
        else:
            found = dict(zip(offsets, [*rest_slabs, *top_slabs]))
            parts = [found[k] for k in range(size)]
        sums += cycle_reduce(parts, size, way)
    (total,) = kernel(close_kernel, sums, [((lang_grp, share, units), f32)], final=True)
    return total.transpose(1, 0, 2)


def solution(mesh):
    in_specs = (
        P(("grp", "seq"), None),
        P(("grp", "seq"), None),
        P(("grp", "seq"), None),
        P(("grp", "seq"), None),
        P(),
        P(("grp", "seq")),
        P("grp", "seq", None),
        P("grp", None, "seq"),
        P("grp", None),
        P(("grp", "seq"), None),
    )
    out_specs = P("seq", "grp", None)

    return jax.shard_map(body, mesh=mesh, in_specs=in_specs, out_specs=out_specs, check_vma=False)
```
